32 devices in a mesh: groups: 2 (over x), utt: 16 (over z, y, core).
Axes of the slice: x: 2, y: 2, z: 4, core: 2. Of those that a mesh axis runs over, the one named last changes fastest.
Arguments:
- cache_kv: bfloat16 [512, 8, 3072], P(('groups', 'utt')), parts along dimension 0, may hold values from -160 to 160
- new_rows: bfloat16 [512, 4608], P(('groups', 'utt')), parts along dimension 0, may hold values from -6 to 6
- cross_queries: bfloat16 [512, 1536], P(('groups', 'utt')), parts along dimension 0, may hold values from -6 to 6
- enc_kv: bfloat16 [32, 256, 3072], P(('groups', 'utt')), parts along dimension 0, may hold values from -160 to 160
- lengths: int32 [32], P(('groups', 'utt')), parts along dimension 0, may hold values from 64 to 256, as said below
- parents: int32 [32, 16], P(('groups', 'utt')), parts along dimension 0, may hold values from 0 to 15
Outputs:
- mixed: bfloat16 [512, 1536], P(('groups', 'utt')), parts along dimension 0
The draws below stay inside these ranges and needn't reach their ends.
There are 2 independent parts, one for each index of `groups`. The reference program is written for one: setup_inputs(seed, part) draws one part's arguments, and reference() takes and returns one part's arrays. A program takes and returns all parts, laid end to end along the dimension named above; each array names one. Nothing has to cross between parts.
Inputs may be any that keep to these rules, and one draw needn't show every extreme that they name: `lengths`: some utterance of each part has all 256 frames.
All inputs are finite; a program needn't handle non-finite values.
Results may differ from the reference program's by a relative error of at most 0.009.
Values may be sent and summed in bfloat16 or wider, within the bound.
A program may use at most 64 MiB of HBM per device.

```python
import jax
import jax.numpy as jnp
from jax import lax

BEAM = 16
HEADS = 12
HD = 128
PREV = 8
FRAMES = 256
FEAT = 1536
ULOC = 1
UTT = 16
HYP = 256
N_UTT = 16


def draw_cache_kv(key, part):
    shape = (HYP, PREV, 2 * FEAT)
    drawn = jax.random.truncated_normal(key, -8.0, 8.0, shape, jnp.float32)
    return drawn.astype(jnp.bfloat16)


def draw_enc_kv(key, part):
    shape = (UTT, FRAMES, 2 * FEAT)
    drawn = jax.random.truncated_normal(key, -8.0, 8.0, shape, jnp.float32)
    return drawn.astype(jnp.bfloat16)


def draw_lengths(key, part):
    spans = jax.random.randint(key, (UTT,), FRAMES // 4, FRAMES + 1)
    longest = jax.random.randint(jax.random.fold_in(key, 17), (), 0, UTT)
    places = lax.broadcasted_iota(jnp.int32, (UTT,), 0)
    return jnp.where(places == longest, FRAMES, spans).astype(jnp.int32)


def set_ends(values, rng, smallest, high):
    shape = values.shape
    spot = [jax.random.randint(jax.random.fold_in(rng, axis), (), 0, shape[axis]) for axis in range(len(shape))]
    values = values.at[tuple(spot)].set(smallest)
    longest = shape.index(max(shape))
    spot[longest] = (spot[longest] + 1) % shape[longest]
    return values.at[tuple(spot)].set(high)


def shard_levels(stream_key, shape, shards, low, high):
    gain = 1.0
    for axis_at, parts in shards:
        draws = jax.random.uniform(jax.random.fold_in(jax.random.fold_in(stream_key, 6), axis_at), (parts,), jnp.float32, low / len(shards), high / len(shards))
        gain = gain * jnp.repeat(jnp.exp(draws), shape[axis_at] // parts).reshape((-1,) + (1,) * (len(shape) - 1 - axis_at))
    return gain


def bell_draw(rng, shape, spread, bound, shards=(), held_as=jnp.bfloat16):
    entries = jax.random.normal(rng, shape, jnp.float32) * spread
    if len(shards) > 0:
        entries = shard_levels(rng, shape, shards, -0.22, 0.18) * entries
    return jnp.clip(entries, min=-bound, max=bound).astype(held_as)


def setup_inputs(seed: int = 0, part: int = 0) -> dict:
    splits = jax.random.split(jax.random.key(seed), 7)
    own_keys = jax.random.split(jax.random.fold_in(splits[6], part), 7)
    cache_kv = draw_cache_kv(jax.random.fold_in(jax.random.fold_in(splits[6], part), 71), part)
    new_rows = bell_draw(own_keys[1], (HYP, 3 * FEAT), 1.0, 6.0, ((0, 16),))
    cross_queries = bell_draw(own_keys[2], (HYP, FEAT), 1.0, 6.0, ((0, 16),))
    enc_kv = draw_enc_kv(jax.random.fold_in(jax.random.fold_in(splits[6], part), 71), part)
    lengths = draw_lengths(jax.random.fold_in(jax.random.fold_in(splits[6], part), 71), part)
    parents = set_ends(jax.random.randint(own_keys[5], (UTT, BEAM), 0, BEAM), jax.random.fold_in(own_keys[5], 1), 0, BEAM - 1).astype(jnp.int32)
    return {"cache_kv": cache_kv, "new_rows": new_rows, "cross_queries": cross_queries, "enc_kv": enc_kv, "lengths": lengths, "parents": parents}


def to_utterance(lm_rows):
    rest = lm_rows.shape[1:]
    grouped = lm_rows.reshape((ULOC, BEAM, N_UTT) + rest)
    order = (2, 0, 1) + tuple(range(3, 3 + len(rest)))
    return jnp.transpose(grouped, order).reshape((ULOC * BEAM * N_UTT,) + rest)


def to_grouped(utt_rows):
    width = utt_rows.shape[1]
    grouped = utt_rows.reshape(N_UTT, ULOC, BEAM, width)
    return jnp.transpose(grouped, (1, 2, 0, 3)).reshape(HYP, width)


def attend_self(query, old_keys, old_values, new_key, new_value):
    row_count = query.shape[0]
    history = old_keys.shape[1]
    scale = HD ** -0.5
    query_heads = query.astype(jnp.float32).reshape(row_count, HEADS, HD)
    key_heads = old_keys.astype(jnp.float32).reshape(row_count, history, HEADS, HD)
    value_heads = old_values.astype(jnp.float32).reshape(row_count, history, HEADS, HD)
    old_scores = jnp.einsum("rhd,rthd->rht", query_heads, key_heads) * scale
    own_score = jnp.einsum("rhd,rhd->rh", query_heads, new_key.astype(jnp.float32).reshape(row_count, HEADS, HD)) * scale
    peak = jnp.maximum(jnp.max(old_scores, axis=2), own_score)
    old_exp = jnp.exp(old_scores - peak[:, :, None])
    own_exp = jnp.exp(own_score - peak)
    total = jnp.sum(old_exp, axis=2) + own_exp
    old_weight = (old_exp / total[:, :, None]).astype(jnp.bfloat16).astype(jnp.float32)
    own_weight = (own_exp / total).astype(jnp.bfloat16).astype(jnp.float32)
    context = jnp.einsum("rht,rthd->rhd", old_weight, value_heads)
    context = context + own_weight[:, :, None] * new_value.astype(jnp.float32).reshape(row_count, HEADS, HD)
    return context.reshape(row_count, HEADS * HD).astype(jnp.bfloat16)


def attend_frames(queries, frames_kv, frame_counts):
    utterances = frame_counts.shape[0]
    frame_total = frames_kv.shape[1]
    scale = HD ** -0.5
    query_heads = queries.astype(jnp.float32).reshape(utterances, BEAM, HEADS, HD)
    key_heads = frames_kv[:, :, :FEAT].astype(jnp.float32).reshape(utterances, frame_total, HEADS, HD)
    value_heads = frames_kv[:, :, FEAT:].astype(jnp.float32).reshape(utterances, frame_total, HEADS, HD)
    scores = jnp.einsum("ubhd,ufhd->uhbf", query_heads, key_heads) * scale
    live = lax.broadcasted_iota(jnp.int32, (utterances, 1, 1, frame_total), 3) < frame_counts[:, None, None, None]
    scores = jnp.where(live, scores, -1e30)
    peak = jnp.max(scores, axis=3, keepdims=True)
    raised = jnp.where(live, jnp.exp(scores - peak), 0.0)
    weights = (raised / jnp.sum(raised, axis=3, keepdims=True)).astype(jnp.bfloat16).astype(jnp.float32)
    context = jnp.einsum("uhbf,ufhd->ubhd", weights, value_heads)
    return context.reshape(utterances * BEAM, HEADS * HD)


def reference(cache_kv, new_rows, cross_queries, enc_kv, lengths, parents):
    cache_u = to_utterance(cache_kv)
    new_u = to_utterance(new_rows)
    grouped = cache_u.reshape(UTT, BEAM, PREV, 2 * FEAT)
    reordered = jax.vmap(lambda block, picks: block[picks])(grouped, parents).reshape(HYP, PREV, 2 * FEAT)
    self_context = attend_self(new_u[:, :FEAT], reordered[:, :, :FEAT], reordered[:, :, FEAT:], new_u[:, FEAT:2 * FEAT], new_u[:, 2 * FEAT:])
    cross_context = attend_frames(cross_queries, enc_kv, lengths)
    mixed_u = (self_context.astype(jnp.float32) + cross_context).astype(jnp.bfloat16)
    return to_grouped(mixed_u)
```

```python
import functools

import jax
import jax.numpy as jnp
from jax import lax
from jax.experimental import pallas as pl
from jax.experimental.pallas import tpu as pltpu
from jax.sharding import PartitionSpec as P

HD = 128
CORES = 2
LINES = 2
PARTS = 3
LOW = -1e30


def contract_last(a, b):
    return lax.dot_general(a, b, (((1,), (1,)), ((), ())), preferred_element_type=jnp.float32)


def fast_kernel(
    n,
    cache_ref, new_ref, cq_ref, enc_ref, len_ref, par_ref,
    out_ref,
    qbuf, kbuf, vbuf, newbuf, cqbuf, encbuf, ptab, ctx, ybuf, sbuf, zbuf, xsend, xrecv,
    local_sem, q_send, q_recv, f_send, c_send, c_recv, p_send, p_recv, x_send, x_recv,
    y_send, y_recv, z_send, z_recv,
):
    feature = cq_ref.shape[1]
    half = feature // CORES
    heads = half // HD
    rows = cq_ref.shape[0]
    utts = new_ref.shape[0]
    old = cache_ref.shape[0]
    history = old // utts
    depth = n // (CORES * LINES)
    scale = HD ** (-0.5)

    me = lax.axis_index("utt")
    z = me // (CORES * LINES)
    y = (me // CORES) % LINES
    c = me % CORES
    y_other = 1 - y
    c_other = 1 - c

    def at(zz, yy, cc):
        return (zz * LINES + yy) * CORES + cc

    def remote(src, dst, ssem, rsem, dev):
        return pltpu.make_async_remote_copy(
            src_ref=src, dst_ref=dst, send_sem=ssem, recv_sem=rsem,
            device_id={"utt": dev}, device_id_type=pl.DeviceIdType.MESH,
        )

    barrier = pltpu.get_barrier_semaphore()
    for k in range(1, n):
        pl.semaphore_signal(
            barrier, inc=1, device_id={"utt": lax.rem(me + k, n)},
            device_id_type=pl.DeviceIdType.MESH,
        )

    my_half = pl.ds(pl.multiple_of(c * half, HD), half)
    my_values = pl.ds(pl.multiple_of(feature + c * half, HD), half)
    my_rows = pl.ds(pl.multiple_of(c * old, old), old)
    copies = [
        pltpu.make_async_copy(cq_ref, cqbuf, local_sem.at[0]),
        pltpu.make_async_copy(enc_ref.at[0], encbuf, local_sem.at[1]),
        pltpu.make_async_copy(new_ref, newbuf, local_sem.at[2]),
        pltpu.make_async_copy(new_ref.at[:, my_half], qbuf.at[z, y, c], local_sem.at[3]),
        pltpu.make_async_copy(cache_ref.at[:, my_half], kbuf.at[my_rows], local_sem.at[4]),
        pltpu.make_async_copy(cache_ref.at[:, my_values], vbuf.at[my_rows], local_sem.at[5]),
        pltpu.make_async_copy(par_ref, ptab.at[me], local_sem.at[6]),
    ]
    for cp in copies:
        cp.start()

    pl.semaphore_wait(barrier, n - 1)

    sends = []
    slot = 0
    for dz in (2, 1, 3, 0):
        zz = lax.rem(z + dz, depth)
        for dc in range(CORES):
            cc = lax.rem(c + dc, CORES)
            cols = pl.ds(pl.multiple_of(cc * half, HD), half)
            for yy in (y, y_other) if dz == 0 else (y,):
                if dz == 0 and dc == 0 and yy is y:
                    continue
                cp = remote(new_ref.at[:, cols], qbuf.at[z, y, c], q_send.at[slot],
                            q_recv.at[me], at(zz, yy, cc))
                cp.start()
                sends.append(cp)
                slot += 1
    for k in range(1, n):
        dev = lax.rem(me + k, n)
        cp = remote(par_ref, ptab.at[me], p_send.at[k - 1], p_recv.at[me], dev)
        cp.start()
        sends.append(cp)
    other_half = pl.ds(pl.multiple_of(c_other * half, HD), half)
    other_values = pl.ds(pl.multiple_of(feature + c_other * half, HD), half)
    partner = at(z, y, c_other)
    cache_in = []
    for i, (cols, buf) in enumerate(((other_half, kbuf), (other_values, vbuf))):
        cp = remote(cache_ref.at[:, cols], buf.at[my_rows], c_send.at[i], c_recv.at[i], partner)
        cp.start()
        sends.append(cp)
        cache_in.append(cp)

    copies[0].wait()
    copies[1].wait()

    frames = encbuf.shape[0]
    live = lax.broadcasted_iota(jnp.int32, (rows, frames), 1) < len_ref[0]
    ones_f = jnp.ones((frames, HD), jnp.bfloat16)

    def cross(h):
        cols = slice(h * HD, (h + 1) * HD)
        s = contract_last(cqbuf[:, cols], encbuf[:, cols]) * scale
        s = jnp.where(live, s, LOW)
        p = jnp.where(live, jnp.exp(s - jnp.max(s, axis=1, keepdims=True)), 0.0).astype(jnp.bfloat16)
        v = jnp.concatenate([encbuf[:, feature + h * HD : feature + (h + 1) * HD], ones_f], axis=1)
        o = jnp.dot(p, v, preferred_element_type=jnp.float32)
        o = o[:, :HD] / o[:, HD:]
        for b in range(rows):
            xsend[b, :, cols] = o[b : b + 1, :]

    for h in range(feature // HD):
        cross(h)

    own_x = pltpu.make_async_copy(xsend.at[me], xrecv.at[me], local_sem.at[7])
    own_x.start()
    for k in range(1, n):
        dev = lax.rem(me + k, n)
        cp = remote(xsend.at[dev], xrecv.at[me], x_send.at[k - 1], x_recv.at[me], dev)
        cp.start()
        sends.append(cp)

    copies[3].wait()
    slot = 0
    for dz in (1, 3, 2):
        zz = lax.rem(z + dz, depth)
        for cc in range(CORES):
            src = at(zz, y, cc)
            piece = qbuf.at[zz, y, cc]
            remote(piece, piece, f_send.at[slot], q_recv.at[src], src).wait_recv()
            cp = remote(piece, piece, f_send.at[slot], q_recv.at[src], at(z, y_other, c))
            cp.start()
            sends.append(cp)
            slot += 1
    piece = qbuf.at[z, y, c_other]
    remote(piece, piece, f_send.at[0], q_recv.at[partner], partner).wait_recv()

    copies[4].wait()
    copies[5].wait()
    for cp in cache_in:
        cp.wait_recv()
    copies[6].wait()
    for k in range(1, n):
        src = lax.rem(me + n - k, n)
        remote(par_ref, ptab.at[src], p_send.at[0], p_recv.at[src], src).wait_recv()

    table = jnp.concatenate([ptab[u] for u in range(utts)], axis=0)
    beam_lane = lax.broadcasted_iota(jnp.int32, table.shape, 1)
    row_u = lax.broadcasted_iota(jnp.int32, (utts, 1), 0)
    chip = me // CORES
    keys = CORES * old
    ones_k = jnp.ones((keys, HD), jnp.bfloat16)

    def partial(yy):
        target = []
        for zz in range(depth):
            for cc in range(CORES):
                col = jnp.sum(jnp.where(beam_lane == at(zz, yy, cc), table, 0), axis=1, keepdims=True)
                target.append((col - chip * CORES) * utts + row_u)
        target = jnp.concatenate(target, axis=0)
        count = depth * CORES * utts
        valid = lax.broadcasted_iota(jnp.int32, (count, keys), 1) // history == target
        sel = jnp.broadcast_to((target >= 0) & (target < CORES * utts), (count, HD))
        lane = lax.broadcasted_iota(jnp.int32, (count, HD), 1)
        stats = jnp.zeros((count, HD), jnp.float32)
        for h in range(heads):
            cols = slice(h * HD, (h + 1) * HD)
            q = qbuf[:, pl.ds(yy, 1), :, :, cols].reshape(count, HD)
            s = jnp.where(valid, contract_last(q, kbuf[:, cols]) * scale, LOW)
            m = jnp.max(s, axis=1, keepdims=True)
            p = jnp.where(valid, jnp.exp(s - m), 0.0).astype(jnp.bfloat16)
            v = jnp.concatenate([vbuf[:, cols], ones_k], axis=1)
            o = jnp.dot(p, v, preferred_element_type=jnp.float32)
            total = jnp.where(sel, o[:, HD:], 1.0)
            ctx[:, pl.ds(yy, 1), :, :, cols] = (o[:, :HD] / total).astype(jnp.bfloat16).reshape(
                depth, 1, CORES, utts, HD)
            rest = jnp.where(sel, m + jnp.log(total), 0.0)
            for k in range(PARTS):
                part = rest.astype(jnp.bfloat16).astype(jnp.float32)
                stats = jnp.where(lane == PARTS * h + k, part, stats)
                rest = rest - part
        ctx[:, pl.ds(yy, 1), :, :, half:] = stats.astype(jnp.bfloat16).reshape(
            depth, 1, CORES, utts, HD)

    partial(y)

    for zz in range(depth):
        for cc in range(CORES):
            src = at(zz, y_other, cc)
            piece = qbuf.at[zz, y_other, cc]
            remote(piece, piece, f_send.at[0], q_recv.at[src], src).wait_recv()
    partial(y_other)

    across = at(z, y_other, c)
    y_in = []
    for dz in (2, 1, 3, 0):
        zz = lax.rem(z + dz, depth)
        cp = remote(ctx.at[zz, y_other], ybuf.at[dz], y_send.at[dz], y_recv.at[dz], across)
        cp.start()
        sends.append(cp)
        y_in.append((dz, zz, cp))

    copies[2].wait()
    own = []
    for h in range(feature // HD):
        q = newbuf[:, h * HD : (h + 1) * HD].astype(jnp.float32)
        k = newbuf[:, feature + h * HD : feature + (h + 1) * HD].astype(jnp.float32)
        own.append(jnp.sum(q * k, axis=1, keepdims=True) * scale)

    slot = 0
    for dz, zz, cp in y_in:
        cp.wait_recv()
        sbuf[dz] = (ctx[pl.ds(zz, 1), pl.ds(y, 1)].reshape(CORES, utts, half + HD) + ybuf[dz])
        for dc in range(CORES):
            cc = lax.rem(c + dc, CORES)
            if dz == 0 and dc == 0:
                stay = pltpu.make_async_copy(sbuf.at[dz, cc], zbuf.at[z, c], local_sem.at[8])
                stay.start()
                continue
            cp = remote(sbuf.at[dz, cc], zbuf.at[z, c], z_send.at[slot], z_recv.at[z * CORES + c],
                        at(zz, y, cc))
            cp.start()
            sends.append(cp)
            slot += 1

    own_x.wait()
    for k in range(1, n):
        src = lax.rem(me + n - k, n)
        remote(xsend.at[src], xrecv.at[src], x_send.at[0], x_recv.at[src], src).wait_recv()

    stay.wait()
    for dz in range(depth):
        zz = lax.rem(z + dz, depth)
        for dc in range(CORES):
            if dz == 0 and dc == 0:
                continue
            cc = lax.rem(c + dc, CORES)
            remote(zbuf.at[zz, cc], zbuf.at[zz, cc], z_send.at[0], z_recv.at[zz * CORES + cc],
                   at(zz, y, cc)).wait_recv()

    for cc in range(CORES):
        both = zbuf[0, cc].astype(jnp.float32)
        for zz in range(1, depth):
            both = both + zbuf[zz, cc].astype(jnp.float32)
        stats = both[:, half:]
        lane = lax.broadcasted_iota(jnp.int32, stats.shape, 1)
        for hl in range(heads):
            h = cc * heads + hl
            cols = slice(h * HD, (h + 1) * HD)
            mine = (lane >= PARTS * hl) & (lane < PARTS * (hl + 1))
            lse = jnp.sum(jnp.where(mine, stats, 0.0), axis=1, keepdims=True)
            peak = jnp.maximum(lse, own[h])
            w_old = jnp.exp(lse - peak)
            w_own = jnp.exp(own[h] - peak)
            inv = 1.0 / (w_old + w_own)
            value = newbuf[:, 2 * feature + h * HD : 2 * feature + (h + 1) * HD].astype(jnp.float32)
            self_ctx = both[:, hl * HD : (hl + 1) * HD] * (w_old * inv) + value * (w_own * inv)
            crossed = jnp.concatenate([xrecv[u, :, cols] for u in range(utts)], axis=0)
            out_ref[:, cols] = (
                self_ctx.astype(jnp.bfloat16).astype(jnp.float32) + crossed
            ).astype(jnp.bfloat16)

    for cp in sends:
        cp.wait_send()


def fast_body(n, cache_kv, new_rows, cross_queries, enc_kv, lengths, parents):
    rows, feature = cross_queries.shape
    utts, history, width = cache_kv.shape
    half = feature // CORES
    old = utts * history
    depth = n // (CORES * LINES)
    frames = enc_kv.shape[1]
    bf = jnp.bfloat16
    dma = pltpu.SemaphoreType.DMA
    hbm = pl.BlockSpec(memory_space=pl.ANY)
    return pl.pallas_call(
        functools.partial(fast_kernel, n),
        out_shape=jax.ShapeDtypeStruct((utts, feature), bf),
        in_specs=[hbm, hbm, hbm, hbm, pl.BlockSpec(memory_space=pltpu.SMEM),
                  pl.BlockSpec(memory_space=pltpu.VMEM)],
        out_specs=pl.BlockSpec(memory_space=pltpu.VMEM),
        scratch_shapes=[
            pltpu.VMEM((depth, LINES, CORES, utts, half), bf),
            pltpu.VMEM((CORES * old, half), bf),
            pltpu.VMEM((CORES * old, half), bf),
            pltpu.VMEM(new_rows.shape, bf),
            pltpu.VMEM(cross_queries.shape, bf),
            pltpu.VMEM((frames, width), bf),
            pltpu.VMEM((n,) + parents.shape, jnp.int32),
            pltpu.VMEM((depth, LINES, CORES, utts, half + HD), bf),
            pltpu.VMEM((depth, CORES, utts, half + HD), bf),
            pltpu.VMEM((depth, CORES, utts, half + HD), bf),
            pltpu.VMEM((depth, CORES, utts, half + HD), bf),
            pltpu.VMEM((rows, 1, feature), jnp.float32),
            pltpu.VMEM((utts, 1, feature), jnp.float32),
            dma((9,)),
            dma((depth * CORES + 1,)), dma((n,)), dma(((depth - 1) * CORES,)),
            dma((2,)), dma((2,)),
            dma((n - 1,)), dma((n,)), dma((n - 1,)), dma((n,)),
            dma((depth,)), dma((depth,)), dma((depth * CORES - 1,)), dma((depth * CORES,)),
        ],
        compiler_params=pltpu.CompilerParams(
            collective_id=0, has_side_effects=True, vmem_limit_bytes=48 << 20
        ),
    )(cache_kv.reshape(old, width), new_rows, cross_queries, enc_kv, lengths, parents)


def reorder(cache_rows, parents):
    utterances, beam_width = parents.shape
    grouped = cache_rows.reshape(utterances, beam_width, cache_rows.shape[1], cache_rows.shape[2])
    picked = jax.vmap(lambda block, picks: block[picks])(grouped, parents)
    return picked.reshape(cache_rows.shape)


def attend_self(query, old_keys, old_values, new_key, new_value):
    row_count = query.shape[0]
    history = old_keys.shape[1]
    head_count = query.shape[1] // HD
    scale = HD ** (-0.5)
    query_heads = query.reshape(row_count, head_count, HD)
    key_heads = old_keys.reshape(row_count, history, head_count, HD)
    value_heads = old_values.reshape(row_count, history, head_count, HD)
    old_scores = (
        jnp.einsum("rhd,rthd->rht", query_heads, key_heads, preferred_element_type=jnp.float32)
        * scale
    )
    own_score = (
        jnp.einsum(
            "rhd,rhd->rh",
            query_heads,
            new_key.reshape(row_count, head_count, HD),
            preferred_element_type=jnp.float32,
        )
        * scale
    )
    peak = jnp.maximum(jnp.max(old_scores, axis=2), own_score)
    old_exp = jnp.exp(old_scores - peak[:, :, None])
    own_exp = jnp.exp(own_score - peak)
    total = jnp.sum(old_exp, axis=2) + own_exp
    old_weight = (old_exp / total[:, :, None]).astype(jnp.bfloat16)
    own_weight = (own_exp / total).astype(jnp.bfloat16)
    context = jnp.einsum(
        "rht,rthd->rhd", old_weight, value_heads, preferred_element_type=jnp.float32
    )
    context = context + own_weight.astype(jnp.float32)[:, :, None] * new_value.reshape(
        row_count, head_count, HD
    ).astype(jnp.float32)
    return context.reshape(row_count, head_count * HD).astype(jnp.bfloat16)


def attend_frames(queries, frames_kv, frame_counts):
    utterances = frame_counts.shape[0]
    beam_width = queries.shape[0] // utterances
    feature = queries.shape[1]
    head_count = feature // HD
    frame_total = frames_kv.shape[1]
    scale = HD ** (-0.5)
    query_heads = queries.reshape(utterances, beam_width, head_count, HD)
    key_heads = frames_kv[:, :, :feature].reshape(utterances, frame_total, head_count, HD)
    value_heads = frames_kv[:, :, feature:].reshape(utterances, frame_total, head_count, HD)
    scores = (
        jnp.einsum("ubhd,ufhd->uhbf", query_heads, key_heads, preferred_element_type=jnp.float32)
        * scale
    )
    live = (
        lax.broadcasted_iota(jnp.int32, (utterances, 1, 1, frame_total), 3)
        < frame_counts[:, None, None, None]
    )
    scores = jnp.where(live, scores, -1e30)
    peak = jnp.max(scores, axis=3, keepdims=True)
    raised = jnp.where(live, jnp.exp(scores - peak), 0.0)
    weights = (raised / jnp.sum(raised, axis=3, keepdims=True)).astype(jnp.bfloat16)
    context = jnp.einsum(
        "uhbf,ufhd->ubhd", weights, value_heads, preferred_element_type=jnp.float32
    )
    return context.reshape(utterances * beam_width, feature)


def body(cache_kv, new_rows, cross_queries, enc_kv, lengths, parents):
    feature = cross_queries.shape[1]
    cross_context = attend_frames(cross_queries, enc_kv, lengths)
    arrived, new_here = (
        lax.all_to_all(cache_kv, "utt", split_axis=0, concat_axis=0, tiled=True),
        lax.all_to_all(new_rows, "utt", split_axis=0, concat_axis=0, tiled=True),
    )
    reordered = reorder(arrived, parents)
    self_context = attend_self(
        new_here[:, :feature],
        reordered[:, :, :feature],
        reordered[:, :, feature:],
        new_here[:, feature : 2 * feature],
        new_here[:, 2 * feature :],
    )
    mixed_here = (self_context.astype(jnp.float32) + cross_context).astype(jnp.bfloat16)
    mixed = lax.all_to_all(mixed_here, "utt", split_axis=0, concat_axis=0, tiled=True)
    return mixed


def solution(mesh):
    placed = (
        P(("groups", "utt"), None, None),
        P(("groups", "utt"), None),
        P(("groups", "utt"), None),
        P(("groups", "utt"), None, None),
        P(("groups", "utt")),
        P(("groups", "utt"), None),
    )
    n = mesh.shape["utt"]

    def either(cache_kv, new_rows, cross_queries, enc_kv, lengths, parents):
        feature = cross_queries.shape[1]
        fits = (
            parents.shape == (1, n)
            and cache_kv.shape[0] == n
            and n == 4 * CORES * LINES
            and feature % (CORES * HD) == 0
            and PARTS * (feature // (CORES * HD)) <= HD
        )
        run = functools.partial(fast_body, n) if fits else body
        return run(cache_kv, new_rows, cross_queries, enc_kv, lengths, parents)

    return jax.shard_map(
        either, mesh=mesh, in_specs=placed, out_specs=P(("groups", "utt"), None), check_vma=False
    )
```

```python
import functools

import jax
import jax.numpy as jnp
from jax import lax
from jax.experimental import pallas as pl
from jax.experimental.pallas import tpu as pltpu
from jax.sharding import PartitionSpec as P

HD = 128
CORES = 2
LINES = 2
PARTS = 3
LOW = -1e30


def contract_last(a, b):
    return lax.dot_general(a, b, (((1,), (1,)), ((), ())), preferred_element_type=jnp.float32)


def fast_kernel(
    n,
    cache_ref, new_ref, cq_ref, enc_ref, len_ref, par_ref,
    out_ref,
    qbuf, kbuf, vbuf, newbuf, cqbuf, encbuf, ptab, ctx, ybuf, sbuf, zbuf, xsend, xrecv,
    local_sem, q_send, q_recv, f_send, c_send, c_recv, p_send, p_recv, x_send, x_recv,
    y_send, y_recv, z_send, z_recv,
):
    feature = cq_ref.shape[1]
    half = feature // CORES
    heads = half // HD
    rows = cq_ref.shape[0]
    utts = new_ref.shape[0]
    old = cache_ref.shape[0]
    history = old // utts
    depth = n // (CORES * LINES)
    scale = HD ** (-0.5)

    me = lax.axis_index("utt")
    z = me // (CORES * LINES)
    y = (me // CORES) % LINES
    c = me % CORES
    y_other = 1 - y
    c_other = 1 - c

    def at(zz, yy, cc):
        return (zz * LINES + yy) * CORES + cc

    def remote(src, dst, ssem, rsem, dev):
        return pltpu.make_async_remote_copy(
            src_ref=src, dst_ref=dst, send_sem=ssem, recv_sem=rsem,
            device_id={"utt": dev}, device_id_type=pl.DeviceIdType.MESH,
        )

    barrier = pltpu.get_barrier_semaphore()
    for k in range(1, n):
        pl.semaphore_signal(
            barrier, inc=1, device_id={"utt": lax.rem(me + k, n)},
            device_id_type=pl.DeviceIdType.MESH,
        )

    my_half = pl.ds(pl.multiple_of(c * half, HD), half)
    my_values = pl.ds(pl.multiple_of(feature + c * half, HD), half)
    my_rows = pl.ds(pl.multiple_of(c * old, old), old)
    copies = [
        pltpu.make_async_copy(cq_ref, cqbuf, local_sem.at[0]),
        pltpu.make_async_copy(enc_ref.at[0], encbuf, local_sem.at[1]),
        pltpu.make_async_copy(new_ref, newbuf, local_sem.at[2]),
        pltpu.make_async_copy(new_ref.at[:, my_half], qbuf.at[z, y, c], local_sem.at[3]),
        pltpu.make_async_copy(cache_ref.at[:, my_half], kbuf.at[my_rows], local_sem.at[4]),
        pltpu.make_async_copy(cache_ref.at[:, my_values], vbuf.at[my_rows], local_sem.at[5]),
        pltpu.make_async_copy(par_ref, ptab.at[me], local_sem.at[6]),
    ]
    for cp in copies:
        cp.start()

    pl.semaphore_wait(barrier, n - 1)

    sends = []
    slot = 0
    for dz in (*range(1, depth), 0):
        zz = lax.rem(z + dz, depth)
        for dc in range(CORES):
            cc = lax.rem(c + dc, CORES)
            cols = pl.ds(pl.multiple_of(cc * half, HD), half)
            for yy in (y, y_other) if dz == 0 else (y,):
                if dz == 0 and dc == 0 and yy is y:
                    continue
                cp = remote(new_ref.at[:, cols], qbuf.at[z, y, c], q_send.at[slot],
                            q_recv.at[me], at(zz, yy, cc))
                cp.start()
                sends.append(cp)
                slot += 1
    for k in range(1, n):
        dev = lax.rem(me + k, n)
        cp = remote(par_ref, ptab.at[me], p_send.at[k - 1], p_recv.at[me], dev)
        cp.start()
        sends.append(cp)
    other_half = pl.ds(pl.multiple_of(c_other * half, HD), half)
    other_values = pl.ds(pl.multiple_of(feature + c_other * half, HD), half)
    partner = at(z, y, c_other)
    cache_in = []
    for i, (cols, buf) in enumerate(((other_half, kbuf), (other_values, vbuf))):
        cp = remote(cache_ref.at[:, cols], buf.at[my_rows], c_send.at[i], c_recv.at[i], partner)
        cp.start()
        sends.append(cp)
        cache_in.append(cp)

    copies[0].wait()
    copies[1].wait()

    frames = encbuf.shape[0]
    live = lax.broadcasted_iota(jnp.int32, (rows, frames), 1) < len_ref[0]
    ones_f = jnp.ones((frames, HD), jnp.bfloat16)

    def cross(h):
        cols = slice(h * HD, (h + 1) * HD)
        s = contract_last(cqbuf[:, cols], encbuf[:, cols]) * scale
        s = jnp.where(live, s, LOW)
        p = jnp.where(live, jnp.exp(s - jnp.max(s, axis=1, keepdims=True)), 0.0).astype(jnp.bfloat16)
        v = jnp.concatenate([encbuf[:, feature + h * HD : feature + (h + 1) * HD], ones_f], axis=1)
        o = jnp.dot(p, v, preferred_element_type=jnp.float32)
        o = o[:, :HD] / o[:, HD:]
        for b in range(rows):
            xsend[b, :, cols] = o[b : b + 1, :]

    for h in range(feature // HD):
        cross(h)

    own_x = pltpu.make_async_copy(xsend.at[me], xrecv.at[me], local_sem.at[7])
    own_x.start()
    for k in range(1, n):
        dev = lax.rem(me + k, n)
        cp = remote(xsend.at[dev], xrecv.at[me], x_send.at[k - 1], x_recv.at[me], dev)
        cp.start()
        sends.append(cp)

    copies[3].wait()
    slot = 0
    for dz in range(1, depth):
        zz = lax.rem(z + dz, depth)
        for cc in range(CORES):
            src = at(zz, y, cc)
            piece = qbuf.at[zz, y, cc]
            remote(piece, piece, f_send.at[slot], q_recv.at[src], src).wait_recv()
            cp = remote(piece, piece, f_send.at[slot], q_recv.at[src], at(z, y_other, c))
            cp.start()
            sends.append(cp)
            slot += 1
    piece = qbuf.at[z, y, c_other]
    remote(piece, piece, f_send.at[0], q_recv.at[partner], partner).wait_recv()

    copies[4].wait()
    copies[5].wait()
    for cp in cache_in:
        cp.wait_recv()
    copies[6].wait()
    for k in range(1, n):
        src = lax.rem(me + n - k, n)
        remote(par_ref, ptab.at[src], p_send.at[0], p_recv.at[src], src).wait_recv()

    table = jnp.concatenate([ptab[u] for u in range(utts)], axis=0)
    beam_lane = lax.broadcasted_iota(jnp.int32, table.shape, 1)
    row_u = lax.broadcasted_iota(jnp.int32, (utts, 1), 0)
    chip = me // CORES
    keys = CORES * old
    ones_k = jnp.ones((keys, HD), jnp.bfloat16)

    def partial(yy):
        target = []
        for zz in range(depth):
            for cc in range(CORES):
                col = jnp.sum(jnp.where(beam_lane == at(zz, yy, cc), table, 0), axis=1, keepdims=True)
                target.append((col - chip * CORES) * utts + row_u)
        target = jnp.concatenate(target, axis=0)
        count = depth * CORES * utts
        valid = lax.broadcasted_iota(jnp.int32, (count, keys), 1) // history == target
        sel = jnp.broadcast_to((target >= 0) & (target < CORES * utts), (count, HD))
        lane = lax.broadcasted_iota(jnp.int32, (count, HD), 1)
        stats = jnp.zeros((count, HD), jnp.float32)
        for h in range(heads):
            cols = slice(h * HD, (h + 1) * HD)
            q = qbuf[:, pl.ds(yy, 1), :, :, cols].reshape(count, HD)
            s = jnp.where(valid, contract_last(q, kbuf[:, cols]) * scale, LOW)
            m = jnp.max(s, axis=1, keepdims=True)
            p = jnp.where(valid, jnp.exp(s - m), 0.0).astype(jnp.bfloat16)
            v = jnp.concatenate([vbuf[:, cols], ones_k], axis=1)
            o = jnp.dot(p, v, preferred_element_type=jnp.float32)
            total = jnp.where(sel, o[:, HD:], 1.0)
            ctx[:, pl.ds(yy, 1), :, :, cols] = (o[:, :HD] / total).astype(jnp.bfloat16).reshape(
                depth, 1, CORES, utts, HD)
            rest = jnp.where(sel, m + jnp.log(total), 0.0)
            for k in range(PARTS):
                part = rest.astype(jnp.bfloat16).astype(jnp.float32)
                stats = jnp.where(lane == PARTS * h + k, part, stats)
                rest = rest - part
        ctx[:, pl.ds(yy, 1), :, :, half:] = stats.astype(jnp.bfloat16).reshape(
            depth, 1, CORES, utts, HD)

    partial(y)

    for zz in range(depth):
        for cc in range(CORES):
            src = at(zz, y_other, cc)
            piece = qbuf.at[zz, y_other, cc]
            remote(piece, piece, f_send.at[0], q_recv.at[src], src).wait_recv()
    partial(y_other)

    across = at(z, y_other, c)
    y_in = []
    for dz in (*range(1, depth), 0):
        zz = lax.rem(z + dz, depth)
        cp = remote(ctx.at[zz, y_other], ybuf.at[dz], y_send.at[dz], y_recv.at[dz], across)
        cp.start()
        sends.append(cp)
        y_in.append((dz, zz, cp))

    copies[2].wait()
    own = []
    for h in range(feature // HD):
        q = newbuf[:, h * HD : (h + 1) * HD].astype(jnp.float32)
        k = newbuf[:, feature + h * HD : feature + (h + 1) * HD].astype(jnp.float32)
        own.append(jnp.sum(q * k, axis=1, keepdims=True) * scale)

    slot = 0
    for dz, zz, cp in y_in:
        cp.wait_recv()
        sbuf[dz] = (ctx[pl.ds(zz, 1), pl.ds(y, 1)].reshape(CORES, utts, half + HD) + ybuf[dz])
        for dc in range(CORES):
            cc = lax.rem(c + dc, CORES)
            if dz == 0 and dc == 0:
                stay = pltpu.make_async_copy(sbuf.at[dz, cc], zbuf.at[z, c], local_sem.at[8])
                stay.start()
                continue
            cp = remote(sbuf.at[dz, cc], zbuf.at[z, c], z_send.at[slot], z_recv.at[z * CORES + c],
                        at(zz, y, cc))
            cp.start()
            sends.append(cp)
            slot += 1

    own_x.wait()
    for k in range(1, n):
        src = lax.rem(me + n - k, n)
        remote(xsend.at[src], xrecv.at[src], x_send.at[0], x_recv.at[src], src).wait_recv()

    stay.wait()
    for dz in range(depth):
        zz = lax.rem(z + dz, depth)
        for dc in range(CORES):
            if dz == 0 and dc == 0:
                continue
            cc = lax.rem(c + dc, CORES)
            remote(zbuf.at[zz, cc], zbuf.at[zz, cc], z_send.at[0], z_recv.at[zz * CORES + cc],
                   at(zz, y, cc)).wait_recv()

    for cc in range(CORES):
        both = zbuf[0, cc].astype(jnp.float32)
        for zz in range(1, depth):
            both = both + zbuf[zz, cc].astype(jnp.float32)
        stats = both[:, half:]
        lane = lax.broadcasted_iota(jnp.int32, stats.shape, 1)
        for hl in range(heads):
            h = cc * heads + hl
            cols = slice(h * HD, (h + 1) * HD)
            mine = (lane >= PARTS * hl) & (lane < PARTS * (hl + 1))
            lse = jnp.sum(jnp.where(mine, stats, 0.0), axis=1, keepdims=True)
            peak = jnp.maximum(lse, own[h])
            w_old = jnp.exp(lse - peak)
            w_own = jnp.exp(own[h] - peak)
            inv = 1.0 / (w_old + w_own)
            value = newbuf[:, 2 * feature + h * HD : 2 * feature + (h + 1) * HD].astype(jnp.float32)
            self_ctx = both[:, hl * HD : (hl + 1) * HD] * (w_old * inv) + value * (w_own * inv)
            crossed = jnp.concatenate([xrecv[u, :, cols] for u in range(utts)], axis=0)
            out_ref[:, cols] = (
                self_ctx.astype(jnp.bfloat16).astype(jnp.float32) + crossed
            ).astype(jnp.bfloat16)

    for cp in sends:
        cp.wait_send()


def fast_body(n, cache_kv, new_rows, cross_queries, enc_kv, lengths, parents):
    rows, feature = cross_queries.shape
    utts, history, width = cache_kv.shape
    half = feature // CORES
    old = utts * history
    depth = n // (CORES * LINES)
    frames = enc_kv.shape[1]
    bf = jnp.bfloat16
    dma = pltpu.SemaphoreType.DMA
    hbm = pl.BlockSpec(memory_space=pl.ANY)
    return pl.pallas_call(
        functools.partial(fast_kernel, n),
        out_shape=jax.ShapeDtypeStruct((utts, feature), bf),
        in_specs=[hbm, hbm, hbm, hbm, pl.BlockSpec(memory_space=pltpu.SMEM),
                  pl.BlockSpec(memory_space=pltpu.VMEM)],
        out_specs=pl.BlockSpec(memory_space=pltpu.VMEM),
        scratch_shapes=[
            pltpu.VMEM((depth, LINES, CORES, utts, half), bf),
            pltpu.VMEM((CORES * old, half), bf),
            pltpu.VMEM((CORES * old, half), bf),
            pltpu.VMEM(new_rows.shape, bf),
            pltpu.VMEM(cross_queries.shape, bf),
            pltpu.VMEM((frames, width), bf),
            pltpu.VMEM((n,) + parents.shape, jnp.int32),
            pltpu.VMEM((depth, LINES, CORES, utts, half + HD), bf),
            pltpu.VMEM((depth, CORES, utts, half + HD), bf),
            pltpu.VMEM((depth, CORES, utts, half + HD), bf),
            pltpu.VMEM((depth, CORES, utts, half + HD), bf),
            pltpu.VMEM((rows, 1, feature), jnp.float32),
            pltpu.VMEM((utts, 1, feature), jnp.float32),
            dma((9,)),
            dma((depth * CORES + 1,)), dma((n,)), dma(((depth - 1) * CORES,)),
            dma((2,)), dma((2,)),
            dma((n - 1,)), dma((n,)), dma((n - 1,)), dma((n,)),
            dma((depth,)), dma((depth,)), dma((depth * CORES - 1,)), dma((depth * CORES,)),
        ],
        compiler_params=pltpu.CompilerParams(
            collective_id=0, has_side_effects=True, vmem_limit_bytes=67043328
        ),
    )(cache_kv.reshape(old, width), new_rows, cross_queries, enc_kv, lengths, parents)


def reorder(cache_rows, parents):
    utterances, beam_width = parents.shape
    grouped = cache_rows.reshape(utterances, beam_width, cache_rows.shape[1], cache_rows.shape[2])
    picked = jax.vmap(lambda block, picks: block[picks])(grouped, parents)
    return picked.reshape(cache_rows.shape)


def attend_self(query, old_keys, old_values, new_key, new_value):
    row_count = query.shape[0]
    history = old_keys.shape[1]
    head_count = query.shape[1] // HD
    scale = HD ** (-0.5)
    query_heads = query.reshape(row_count, head_count, HD)
    key_heads = old_keys.reshape(row_count, history, head_count, HD)
    value_heads = old_values.reshape(row_count, history, head_count, HD)
    old_scores = (
        jnp.einsum("rhd,rthd->rht", query_heads, key_heads, preferred_element_type=jnp.float32)
        * scale
    )
    own_score = (
        jnp.einsum(
            "rhd,rhd->rh",
            query_heads,
            new_key.reshape(row_count, head_count, HD),
            preferred_element_type=jnp.float32,
        )
        * scale
    )
    peak = jnp.maximum(jnp.max(old_scores, axis=2), own_score)
    old_exp = jnp.exp(old_scores - peak[:, :, None])
    own_exp = jnp.exp(own_score - peak)
    total = jnp.sum(old_exp, axis=2) + own_exp
    old_weight = (old_exp / total[:, :, None]).astype(jnp.bfloat16)
    own_weight = (own_exp / total).astype(jnp.bfloat16)
    context = jnp.einsum(
        "rht,rthd->rhd", old_weight, value_heads, preferred_element_type=jnp.float32
    )
    context = context + own_weight.astype(jnp.float32)[:, :, None] * new_value.reshape(
        row_count, head_count, HD
    ).astype(jnp.float32)
    return context.reshape(row_count, head_count * HD).astype(jnp.bfloat16)


def attend_frames(queries, frames_kv, frame_counts):
    utterances = frame_counts.shape[0]
    beam_width = queries.shape[0] // utterances
    feature = queries.shape[1]
    head_count = feature // HD
    frame_total = frames_kv.shape[1]
    scale = HD ** (-0.5)
    query_heads = queries.reshape(utterances, beam_width, head_count, HD)
    key_heads = frames_kv[:, :, :feature].reshape(utterances, frame_total, head_count, HD)
    value_heads = frames_kv[:, :, feature:].reshape(utterances, frame_total, head_count, HD)
    scores = (
        jnp.einsum("ubhd,ufhd->uhbf", query_heads, key_heads, preferred_element_type=jnp.float32)
        * scale
    )
    live = (
        lax.broadcasted_iota(jnp.int32, (utterances, 1, 1, frame_total), 3)
        < frame_counts[:, None, None, None]
    )
    scores = jnp.where(live, scores, -1e30)
    peak = jnp.max(scores, axis=3, keepdims=True)
    raised = jnp.where(live, jnp.exp(scores - peak), 0.0)
    weights = (raised / jnp.sum(raised, axis=3, keepdims=True)).astype(jnp.bfloat16)
    context = jnp.einsum(
        "uhbf,ufhd->ubhd", weights, value_heads, preferred_element_type=jnp.float32
    )
    return context.reshape(utterances * beam_width, feature)


def body(cache_kv, new_rows, cross_queries, enc_kv, lengths, parents):
    feature = cross_queries.shape[1]
    cross_context = attend_frames(cross_queries, enc_kv, lengths)
    arrived, new_here = (
        lax.all_to_all(cache_kv, "utt", split_axis=0, concat_axis=0, tiled=True),
        lax.all_to_all(new_rows, "utt", split_axis=0, concat_axis=0, tiled=True),
    )
    reordered = reorder(arrived, parents)
    self_context = attend_self(
        new_here[:, :feature],
        reordered[:, :, :feature],
        reordered[:, :, feature:],
        new_here[:, feature : 2 * feature],
        new_here[:, 2 * feature :],
    )
    mixed_here = (self_context.astype(jnp.float32) + cross_context).astype(jnp.bfloat16)
    mixed = lax.all_to_all(mixed_here, "utt", split_axis=0, concat_axis=0, tiled=True)
    return mixed


def solution(mesh):
    placed = (
        P(("groups", "utt"), None, None),
        P(("groups", "utt"), None),
        P(("groups", "utt"), None),
        P(("groups", "utt"), None, None),
        P(("groups", "utt")),
        P(("groups", "utt"), None),
    )
    n = mesh.shape["utt"]

    def either(cache_kv, new_rows, cross_queries, enc_kv, lengths, parents):
        feature = cross_queries.shape[1]
        fits = (
            parents.shape == (1, n)
            and cache_kv.shape[0] == n
            and n % (CORES * LINES) == 0
            and feature % (CORES * HD) == 0
            and PARTS * (feature // (CORES * HD)) <= HD
        )
        run = functools.partial(fast_body, n) if fits else body
        return run(cache_kv, new_rows, cross_queries, enc_kv, lengths, parents)

    return jax.shard_map(
        either, mesh=mesh, in_specs=placed, out_specs=P(("groups", "utt"), None), check_vma=False
    )
```

```python
import functools

import jax
import jax.numpy as jnp
from jax import lax
from jax.experimental import pallas as pl
from jax.experimental.pallas import tpu as pltpu
from jax.sharding import PartitionSpec as P

HD = 128
CORES = 2
LINES = 2
PARTS = 3
CHUNKS = 2
LOW = -1e30


def contract_last(a, b):
    return lax.dot_general(a, b, (((1,), (1,)), ((), ())), preferred_element_type=jnp.float32)


def fast_kernel(
    n,
    cache_ref, new_ref, cq_ref, enc_ref, len_ref, par_ref,
    out_ref,
    qbuf, kbuf, vbuf, newbuf, cqbuf, encbuf, ptab, ctx, ybuf, sbuf, zbuf, xsend, xrecv,
    local_sem, q_send, q_recv, f_send, c_send, c_recv, p_send, p_recv, x_send, x_recv,
    y_send, y_recv, z_send, z_recv, qown_sem, stay_sem,
):
    feature = cq_ref.shape[1]
    half = feature // CORES
    heads = half // HD
    chunks = CHUNKS if heads % CHUNKS == 0 else 1
    chunk_heads = heads // chunks
    width = chunk_heads * HD
    rows = cq_ref.shape[0]
    utts = new_ref.shape[0]
    old = cache_ref.shape[0]
    history = old // utts
    depth = n // (CORES * LINES)
    scale = HD ** (-0.5)

    me = lax.axis_index("utt")
    z = me // (CORES * LINES)
    y = (me // CORES) % LINES
    c = me % CORES
    y_other = 1 - y
    c_other = 1 - c

    def at(zz, yy, cc):
        return (zz * LINES + yy) * CORES + cc

    def remote(src, dst, ssem, rsem, dev):
        return pltpu.make_async_remote_copy(
            src_ref=src, dst_ref=dst, send_sem=ssem, recv_sem=rsem,
            device_id={"utt": dev}, device_id_type=pl.DeviceIdType.MESH,
        )

    barrier = pltpu.get_barrier_semaphore()
    for k in range(1, n):
        pl.semaphore_signal(
            barrier, inc=1, device_id={"utt": lax.rem(me + k, n)},
            device_id_type=pl.DeviceIdType.MESH,
        )

    def chunk_cols(cc, k):
        return pl.ds(pl.multiple_of(cc * half + k * width, HD), width)

    my_half = pl.ds(pl.multiple_of(c * half, HD), half)
    my_values = pl.ds(pl.multiple_of(feature + c * half, HD), half)
    my_rows = pl.ds(pl.multiple_of(c * old, old), old)
    copies = [
        pltpu.make_async_copy(cq_ref, cqbuf, local_sem.at[0]),
        pltpu.make_async_copy(enc_ref.at[0], encbuf, local_sem.at[1]),
        pltpu.make_async_copy(new_ref, newbuf, local_sem.at[2]),
        pltpu.make_async_copy(cache_ref.at[:, my_half], kbuf.at[my_rows], local_sem.at[4]),
        pltpu.make_async_copy(cache_ref.at[:, my_values], vbuf.at[my_rows], local_sem.at[5]),
        pltpu.make_async_copy(par_ref, ptab.at[me], local_sem.at[6]),
    ] + [
        pltpu.make_async_copy(new_ref.at[:, chunk_cols(c, k)], qbuf.at[k, z, y, c], qown_sem.at[k])
        for k in range(chunks)
    ]
    for cp in copies:
        cp.start()

    copies[0].wait()
    copies[1].wait()

    frames = encbuf.shape[0]
    live = lax.broadcasted_iota(jnp.int32, (rows, frames), 1) < len_ref[0]
    ones_f = jnp.ones((frames, HD), jnp.bfloat16)

    def cross(h):
        cols = slice(h * HD, (h + 1) * HD)
        s = contract_last(cqbuf[:, cols], encbuf[:, cols]) * scale
        s = jnp.where(live, s, LOW)
        p = jnp.where(live, jnp.exp(s - jnp.max(s, axis=1, keepdims=True)), 0.0).astype(jnp.bfloat16)
        v = jnp.concatenate([encbuf[:, feature + h * HD : feature + (h + 1) * HD], ones_f], axis=1)
        o = jnp.dot(p, v, preferred_element_type=jnp.float32)
        o = o[:, :HD] / o[:, HD:]
        for b in range(rows):
            xsend[b, :, cols] = o[b : b + 1, :]

    early = (feature // HD) // 3
    for h in range(early):
        cross(h)

    copies[2].wait()
    pl.semaphore_wait(barrier, n - 1)

    sends = []

    def spread(k):
        slot = 0
        for dz in (*range(1, depth), 0):
            zz = lax.rem(z + dz, depth)
            for dc in range(CORES):
                cc = lax.rem(c + dc, CORES)
                for yy in (y_other, y) if dz == 0 else (y,):
                    if dz == 0 and dc == 0 and yy is y:
                        continue
                    cp = remote(newbuf.at[:, chunk_cols(cc, k)], qbuf.at[k, z, y, c],
                                q_send.at[k, slot], q_recv.at[k, me], at(zz, yy, cc))
                    cp.start()
                    sends.append(cp)
                    slot += 1

    spread(0)
    for k in range(1, n):
        dev = lax.rem(me + k, n)
        cp = remote(par_ref, ptab.at[me], p_send.at[k - 1], p_recv.at[me], dev)
        cp.start()
        sends.append(cp)
    for k in range(1, chunks):
        spread(k)
    other_half = pl.ds(pl.multiple_of(c_other * half, HD), half)
    other_values = pl.ds(pl.multiple_of(feature + c_other * half, HD), half)
    partner = at(z, y, c_other)
    cache_in = []
    for i, (cols, buf) in enumerate(((other_half, kbuf), (other_values, vbuf))):
        cp = remote(cache_ref.at[:, cols], buf.at[my_rows], c_send.at[i], c_recv.at[i], partner)
        cp.start()
        sends.append(cp)
        cache_in.append(cp)

    def forward(k):
        slot = 0
        for dz in range(1, depth):
            zz = lax.rem(z + dz, depth)
            for cc in range(CORES):
                src = at(zz, y, cc)
                piece = qbuf.at[k, zz, y, cc]
                remote(piece, piece, f_send.at[k, slot], q_recv.at[k, src], src).wait_recv()
                cp = remote(piece, piece, f_send.at[k, slot], q_recv.at[k, src], at(z, y_other, c))
                cp.start()
                sends.append(cp)
                slot += 1

    forward(0)

    for h in range(early, feature // HD):
        cross(h)

    own_x = pltpu.make_async_copy(xsend.at[me], xrecv.at[me], local_sem.at[7])
    own_x.start()
    for k in range(1, n):
        dev = lax.rem(me + k, n)
        cp = remote(xsend.at[dev], xrecv.at[me], x_send.at[k - 1], x_recv.at[me], dev)
        cp.start()
        sends.append(cp)

    copies[3].wait()
    copies[4].wait()
    for cp in cache_in:
        cp.wait_recv()
    copies[5].wait()
    for k in range(1, n):
        src = lax.rem(me + n - k, n)
        remote(par_ref, ptab.at[src], p_send.at[0], p_recv.at[src], src).wait_recv()

    table = jnp.concatenate([ptab[u] for u in range(utts)], axis=0)
    beam_lane = lax.broadcasted_iota(jnp.int32, table.shape, 1)
    row_u = lax.broadcasted_iota(jnp.int32, (utts, 1), 0)
    chip = me // CORES
    keys = CORES * old
    ones_k = jnp.ones((keys, HD), jnp.bfloat16)

    def masks(yy):
        target = []
        for zz in range(depth):
            for cc in range(CORES):
                col = jnp.sum(jnp.where(beam_lane == at(zz, yy, cc), table, 0), axis=1, keepdims=True)
                target.append((col - chip * CORES) * utts + row_u)
        target = jnp.concatenate(target, axis=0)
        valid = lax.broadcasted_iota(jnp.int32, (count, keys), 1) // history == target
        sel = jnp.broadcast_to((target >= 0) & (target < CORES * utts), (count, HD))
        return valid, sel

    count = depth * CORES * utts
    lane = lax.broadcasted_iota(jnp.int32, (count, HD), 1)

    def partial(yy, mask, stats, k):
        valid, sel = mask
        for hk in range(chunk_heads):
            h = k * chunk_heads + hk
            cols = slice(h * HD, (h + 1) * HD)
            kcols = slice(hk * HD, (hk + 1) * HD)
            q = qbuf[k, :, pl.ds(yy, 1), :, :, kcols].reshape(count, HD)
            s = jnp.where(valid, contract_last(q, kbuf[:, cols]) * scale, LOW)
            m = jnp.max(s, axis=1, keepdims=True)
            p = jnp.where(valid, jnp.exp(s - m), 0.0).astype(jnp.bfloat16)
            v = jnp.concatenate([vbuf[:, cols], ones_k], axis=1)
            o = jnp.dot(p, v, preferred_element_type=jnp.float32)
            total = jnp.where(sel, o[:, HD:], 1.0)
            ctx[k][:, pl.ds(yy, 1), :, :, kcols] = (o[:, :HD] / total).astype(jnp.bfloat16).reshape(
                depth, 1, CORES, utts, HD)
            rest = jnp.where(sel, m + jnp.log(total), 0.0)
            for j in range(PARTS):
                part = rest.astype(jnp.bfloat16).astype(jnp.float32)
                stats = jnp.where(lane == PARTS * h + j, part, stats)
                rest = rest - part
        if k == chunks - 1:
            ctx[k][:, pl.ds(yy, 1), :, :, width:] = stats.astype(jnp.bfloat16).reshape(
                depth, 1, CORES, utts, HD)
        return stats

    across = at(z, y_other, c)
    y_in = [[] for _ in range(chunks)]

    def turn(k):
        for dz in (*range(1, depth), 0):
            zz = lax.rem(z + dz, depth)
            cp = remote(ctx[k].at[zz, y_other], ybuf[k].at[dz], y_send.at[k, dz], y_recv.at[k, dz],
                        across)
            cp.start()
            sends.append(cp)
            y_in[k].append((dz, zz, cp))

    stays = []

    def deliver(k):
        slot = 0
        for dz, zz, cp in y_in[k]:
            cp.wait_recv()
            sbuf[k][dz] = ctx[k][pl.ds(zz, 1), pl.ds(y, 1)].reshape(sbuf[k].shape[1:]) + ybuf[k][dz]
            for dc in range(CORES):
                cc = lax.rem(c + dc, CORES)
                if dz == 0 and dc == 0:
                    stay = pltpu.make_async_copy(sbuf[k].at[dz, cc], zbuf[k].at[z, c], stay_sem.at[k])
                    stay.start()
                    stays.append(stay)
                    continue
                cp = remote(sbuf[k].at[dz, cc], zbuf[k].at[z, c], z_send.at[k, slot],
                            z_recv.at[k, z * CORES + c], at(zz, y, cc))
                cp.start()
                sends.append(cp)
                slot += 1

    mask_here, mask_there = masks(y), masks(y_other)
    stats_here = stats_there = jnp.zeros((count, HD), jnp.float32)
    for k in range(chunks):
        piece = qbuf.at[k, z, y, c_other]
        remote(piece, piece, f_send.at[k, 0], q_recv.at[k, partner], partner).wait_recv()
        copies[6 + k].wait()
        if k + 1 < chunks:
            forward(k + 1)
        stats_here = partial(y, mask_here, stats_here, k)
        for zz in range(depth):
            for cc in range(CORES):
                src = at(zz, y_other, cc)
                piece = qbuf.at[k, zz, y_other, cc]
                remote(piece, piece, f_send.at[k, 0], q_recv.at[k, src], src).wait_recv()
        stats_there = partial(y_other, mask_there, stats_there, k)
        turn(k)
        if k > 0:
            deliver(k - 1)

    own = []
    for h in range(feature // HD):
        q = newbuf[:, h * HD : (h + 1) * HD].astype(jnp.float32)
        k = newbuf[:, feature + h * HD : feature + (h + 1) * HD].astype(jnp.float32)
        own.append(jnp.sum(q * k, axis=1, keepdims=True) * scale)

    deliver(chunks - 1)

    own_x.wait()
    for k in range(1, n):
        src = lax.rem(me + n - k, n)
        remote(xsend.at[src], xrecv.at[src], x_send.at[0], x_recv.at[src], src).wait_recv()

    for stay in stays:
        stay.wait()
    for k in range(chunks):
        for dz in range(depth):
            zz = lax.rem(z + dz, depth)
            for dc in range(CORES):
                if dz == 0 and dc == 0:
                    continue
                cc = lax.rem(c + dc, CORES)
                remote(zbuf[k].at[zz, cc], zbuf[k].at[zz, cc], z_send.at[k, 0],
                       z_recv.at[k, zz * CORES + cc], at(zz, y, cc)).wait_recv()

    for cc in range(CORES):
        both = []
        for k in range(chunks):
            both.append(zbuf[k][0, cc].astype(jnp.float32))
            for zz in range(1, depth):
                both[k] = both[k] + zbuf[k][zz, cc].astype(jnp.float32)
        both = jnp.concatenate(both, axis=1)
        stats = both[:, half:]
        lane = lax.broadcasted_iota(jnp.int32, stats.shape, 1)
        for hl in range(heads):
            h = cc * heads + hl
            cols = slice(h * HD, (h + 1) * HD)
            mine = (lane >= PARTS * hl) & (lane < PARTS * (hl + 1))
            lse = jnp.sum(jnp.where(mine, stats, 0.0), axis=1, keepdims=True)
            peak = jnp.maximum(lse, own[h])
            w_old = jnp.exp(lse - peak)
            w_own = jnp.exp(own[h] - peak)
            inv = 1.0 / (w_old + w_own)
            value = newbuf[:, 2 * feature + h * HD : 2 * feature + (h + 1) * HD].astype(jnp.float32)
            self_ctx = both[:, hl * HD : (hl + 1) * HD] * (w_old * inv) + value * (w_own * inv)
            crossed = jnp.concatenate([xrecv[u, :, cols] for u in range(utts)], axis=0)
            out_ref[:, cols] = (
                self_ctx.astype(jnp.bfloat16).astype(jnp.float32) + crossed
            ).astype(jnp.bfloat16)

    for cp in sends:
        cp.wait_send()


def fast_body(n, cache_kv, new_rows, cross_queries, enc_kv, lengths, parents):
    rows, feature = cross_queries.shape
    utts, history, width = cache_kv.shape
    half = feature // CORES
    old = utts * history
    depth = n // (CORES * LINES)
    heads = half // HD
    chunks = CHUNKS if heads % CHUNKS == 0 else 1
    w = half // chunks
    wide = [w] * (chunks - 1) + [w + HD]
    frames = enc_kv.shape[1]
    bf = jnp.bfloat16
    dma = pltpu.SemaphoreType.DMA
    hbm = pl.BlockSpec(memory_space=pl.ANY)
    return pl.pallas_call(
        functools.partial(fast_kernel, n),
        out_shape=jax.ShapeDtypeStruct((utts, feature), bf),
        in_specs=[hbm, hbm, hbm, hbm, pl.BlockSpec(memory_space=pltpu.SMEM),
                  pl.BlockSpec(memory_space=pltpu.VMEM)],
        out_specs=pl.BlockSpec(memory_space=pltpu.VMEM),
        scratch_shapes=[
            pltpu.VMEM((chunks, depth, LINES, CORES, utts, w), bf),
            pltpu.VMEM((CORES * old, half), bf),
            pltpu.VMEM((CORES * old, half), bf),
            pltpu.VMEM(new_rows.shape, bf),
            pltpu.VMEM(cross_queries.shape, bf),
            pltpu.VMEM((frames, width), bf),
            pltpu.VMEM((n,) + parents.shape, jnp.int32),
            [pltpu.VMEM((depth, LINES, CORES, utts, v), bf) for v in wide],
            [pltpu.VMEM((depth, CORES, utts, v), bf) for v in wide],
            [pltpu.VMEM((depth, CORES, utts, v), bf) for v in wide],
            [pltpu.VMEM((depth, CORES, utts, v), bf) for v in wide],
            pltpu.VMEM((rows, 1, feature), jnp.float32),
            pltpu.VMEM((utts, 1, feature), jnp.float32),
            dma((8,)),
            dma((chunks, depth * CORES + 1)), dma((chunks, n)), dma((chunks, (depth - 1) * CORES)),
            dma((2,)), dma((2,)),
            dma((n - 1,)), dma((n,)), dma((n - 1,)), dma((n,)),
            dma((chunks, depth)), dma((chunks, depth)),
            dma((chunks, depth * CORES - 1)), dma((chunks, depth * CORES)), dma((chunks,)), dma((chunks,)),
        ],
        compiler_params=pltpu.CompilerParams(
            collective_id=0, has_side_effects=True, vmem_limit_bytes=67043328
        ),
    )(cache_kv.reshape(old, width), new_rows, cross_queries, enc_kv, lengths, parents)


def reorder(cache_rows, parents):
    utterances, beam_width = parents.shape
    grouped = cache_rows.reshape(utterances, beam_width, cache_rows.shape[1], cache_rows.shape[2])
    picked = jax.vmap(lambda block, picks: block[picks])(grouped, parents)
    return picked.reshape(cache_rows.shape)


def attend_self(query, old_keys, old_values, new_key, new_value):
    row_count = query.shape[0]
    history = old_keys.shape[1]
    head_count = query.shape[1] // HD
    scale = HD ** (-0.5)
    query_heads = query.reshape(row_count, head_count, HD)
    key_heads = old_keys.reshape(row_count, history, head_count, HD)
    value_heads = old_values.reshape(row_count, history, head_count, HD)
    old_scores = (
        jnp.einsum("rhd,rthd->rht", query_heads, key_heads, preferred_element_type=jnp.float32)
        * scale
    )
    own_score = (
        jnp.einsum(
            "rhd,rhd->rh",
            query_heads,
            new_key.reshape(row_count, head_count, HD),
            preferred_element_type=jnp.float32,
        )
        * scale
    )
    peak = jnp.maximum(jnp.max(old_scores, axis=2), own_score)
    old_exp = jnp.exp(old_scores - peak[:, :, None])
    own_exp = jnp.exp(own_score - peak)
    total = jnp.sum(old_exp, axis=2) + own_exp
    old_weight = (old_exp / total[:, :, None]).astype(jnp.bfloat16)
    own_weight = (own_exp / total).astype(jnp.bfloat16)
    context = jnp.einsum(
        "rht,rthd->rhd", old_weight, value_heads, preferred_element_type=jnp.float32
    )
    context = context + own_weight.astype(jnp.float32)[:, :, None] * new_value.reshape(
        row_count, head_count, HD
    ).astype(jnp.float32)
    return context.reshape(row_count, head_count * HD).astype(jnp.bfloat16)


def attend_frames(queries, frames_kv, frame_counts):
    utterances = frame_counts.shape[0]
    beam_width = queries.shape[0] // utterances
    feature = queries.shape[1]
    head_count = feature // HD
    frame_total = frames_kv.shape[1]
    scale = HD ** (-0.5)
    query_heads = queries.reshape(utterances, beam_width, head_count, HD)
    key_heads = frames_kv[:, :, :feature].reshape(utterances, frame_total, head_count, HD)
    value_heads = frames_kv[:, :, feature:].reshape(utterances, frame_total, head_count, HD)
    scores = (
        jnp.einsum("ubhd,ufhd->uhbf", query_heads, key_heads, preferred_element_type=jnp.float32)
        * scale
    )
    live = (
        lax.broadcasted_iota(jnp.int32, (utterances, 1, 1, frame_total), 3)
        < frame_counts[:, None, None, None]
    )
    scores = jnp.where(live, scores, -1e30)
    peak = jnp.max(scores, axis=3, keepdims=True)
    raised = jnp.where(live, jnp.exp(scores - peak), 0.0)
    weights = (raised / jnp.sum(raised, axis=3, keepdims=True)).astype(jnp.bfloat16)
    context = jnp.einsum(
        "uhbf,ufhd->ubhd", weights, value_heads, preferred_element_type=jnp.float32
    )
    return context.reshape(utterances * beam_width, feature)


def body(cache_kv, new_rows, cross_queries, enc_kv, lengths, parents):
    feature = cross_queries.shape[1]
    cross_context = attend_frames(cross_queries, enc_kv, lengths)
    arrived, new_here = (
        lax.all_to_all(cache_kv, "utt", split_axis=0, concat_axis=0, tiled=True),
        lax.all_to_all(new_rows, "utt", split_axis=0, concat_axis=0, tiled=True),
    )
    reordered = reorder(arrived, parents)
    self_context = attend_self(
        new_here[:, :feature],
        reordered[:, :, :feature],
        reordered[:, :, feature:],
        new_here[:, feature : 2 * feature],
        new_here[:, 2 * feature :],
    )
    mixed_here = (self_context.astype(jnp.float32) + cross_context).astype(jnp.bfloat16)
    mixed = lax.all_to_all(mixed_here, "utt", split_axis=0, concat_axis=0, tiled=True)
    return mixed


def solution(mesh):
    placed = (
        P(("groups", "utt"), None, None),
        P(("groups", "utt"), None),
        P(("groups", "utt"), None),
        P(("groups", "utt"), None, None),
        P(("groups", "utt")),
        P(("groups", "utt"), None),
    )
    n = mesh.shape["utt"]

    def either(cache_kv, new_rows, cross_queries, enc_kv, lengths, parents):
        feature = cross_queries.shape[1]
        fits = (
            parents.shape == (1, n)
            and cache_kv.shape[0] == n
            and n % (CORES * LINES) == 0
            and feature % (CORES * HD) == 0
            and PARTS * (feature // (CORES * HD)) <= HD
        )
        run = functools.partial(fast_body, n) if fits else body
        return run(cache_kv, new_rows, cross_queries, enc_kv, lengths, parents)

    return jax.shard_map(
        either, mesh=mesh, in_specs=placed, out_specs=P(("groups", "utt"), None), check_vma=False
    )
```
